32 devices in a mesh: patch: 16 (over z, y, core), band: 2 (over x).
Axes of the slice: x: 2, y: 2, z: 4, core: 2. Of those that a mesh axis runs over, the one named last changes fastest.
Arguments:
- latents: float32 [10240, 512], P('patch', 'band'), may hold values from -6 to 6
- edge_latents: float32 [81920, 512], P(('patch', 'band')), may hold values from -6 to 6
- edge_sender: int32 [81920], P(('patch', 'band')), may hold values from 0 to 575, as said below
- edge_receiver: int32 [81920], P(('patch', 'band')), may hold values from 0 to 319
- block_counts: int32 [640], P(('patch', 'band')), may hold values from 16 to 128, as said below
- send_rows: int32 [32, 32, 8], P(('patch', 'band')), may hold values from 0 to 319
- edge_first_weight: bfloat16 [2, 1536, 512], replicated, may hold values from -0.15625 to 0.15625
- edge_first_bias: float32 [2, 512], replicated, may hold values from -3 to 3
- edge_second_weight: bfloat16 [2, 512, 512], replicated
- edge_gain: float32 [2, 512], replicated, may hold values from 0.1 to 1.9
- edge_offset: float32 [2, 512], replicated, may hold values from -3 to 3
- node_first_weight: bfloat16 [2, 1024, 512], replicated, may hold values from -0.1875 to 0.1875
- node_first_bias: float32 [2, 512], replicated, may hold values from -3 to 3
- node_second_weight: bfloat16 [2, 512, 512], replicated
- node_gain: float32 [2, 512], replicated, may hold values from 0.1 to 1.9
- node_offset: float32 [2, 512], replicated, may hold values from -3 to 3
Outputs:
- new_nodes: float32 [10240, 512], P(('patch', 'band'))
- new_edges: float32 [81920, 512], P(('patch', 'band'))
The draws below stay inside these ranges and needn't reach their ends.
Inputs may be any that keep to these rules, and one draw needn't show every extreme that they name: `edge_sender`: an entry below 320 names a node row of the edge's own device; an entry k above names slot (k - 320) % 8 of the rows that device (k - 320) // 8 sends to the edge's device. `block_counts`: the used slots of a block are its first ones; every device has a full block. send_rows[d, q] lists node rows of device d, numbered within d, that device q receives from d.
All inputs are finite; a program needn't handle non-finite values.
Results may differ from the reference program's by a relative error of at most 0.0045.
Values may be sent and summed in bfloat16 or wider, within the bound.
A program may use at most 128 MiB of HBM per device.

```python
import math
import jax
import jax.numpy as jnp
from jax import lax

D = 512
HID = 512
NODE_DEV = 320
BLOCKS = 20
BLOCK = 128
SLOT = 8
LAYERS = 2
SHARDS = 32
NODES = 10240
EDGE_DEV = 2560
EDGES = 81920


def draw_edge_sender(key, part):
    subkeys = jax.random.split(jax.random.fold_in(key, 5), 6)
    shape_two = (SHARDS, EDGE_DEV)
    lower = SLOT // 2 + 1
    counts = lower + jax.random.randint(subkeys[0], (SHARDS, SHARDS), 0, 1 << 20) % (SLOT + 1 - lower)
    fullest = jax.random.randint(subkeys[1], (SHARDS, 1), 0, SHARDS)
    counts = jnp.where(jnp.arange(SHARDS)[None, :] == fullest, SLOT, counts)
    local_rows = jax.random.randint(subkeys[2], shape_two, 0, NODE_DEV)
    source_shard = jax.random.randint(subkeys[3], shape_two, 0, SHARDS)
    spread_bits = jax.random.randint(subkeys[4], shape_two, 0, 1 << 20)
    chosen = jnp.take_along_axis(counts, source_shard, axis=1)
    remote = NODE_DEV + source_shard * SLOT + spread_bits % chosen
    picker = jax.random.randint(subkeys[5], shape_two, 0, 2)
    return jnp.where(picker == 0, local_rows, remote).reshape(-1).astype(jnp.int32)


def draw_block_counts(key, part):
    subkeys = jax.random.split(jax.random.fold_in(key, 7), 3)
    floor_value = max(1, BLOCK // 8)
    device_low = jax.random.randint(subkeys[0], (SHARDS, 1), floor_value, BLOCK + 1)
    raw_bits = jax.random.randint(subkeys[1], (SHARDS, BLOCKS), 0, 1 << 20)
    counts = device_low + raw_bits % (BLOCK + 1 - device_low)
    full_block = jax.random.randint(subkeys[2], (SHARDS, 1), 0, BLOCKS)
    counts = jnp.where(jnp.arange(BLOCKS)[None, :] == full_block, BLOCK, counts)
    return counts.reshape(-1).astype(jnp.int32)


def scaled_weight(key, depth_count, fan_rows, fan_cols):
    subkeys = jax.random.split(key, 2)
    base = jax.random.normal(subkeys[0], (depth_count, fan_rows, fan_cols), jnp.float32)
    column_scale = jnp.exp(jax.random.uniform(subkeys[1], (depth_count, 1, fan_cols), jnp.float32, math.log(0.3), math.log(3.0)))
    return base * column_scale * fan_rows ** (-0.5)


def draw_edge_second_weight(key, part):
    return scaled_weight(jax.random.fold_in(key, 21), LAYERS, HID, D).astype(jnp.bfloat16)


def draw_node_second_weight(key, part):
    return scaled_weight(jax.random.fold_in(key, 23), LAYERS, HID, D).astype(jnp.bfloat16)


def with_ends(array, stream_key, low, top_value):
    longest = array.shape.index(max(array.shape))
    spots = []
    for shift in (0, 1):
        where = [jax.random.randint(jax.random.fold_in(stream_key, axis), (), 0, length) for axis, length in enumerate(array.shape)]
        where[longest] = (where[longest] + shift) % array.shape[longest]
        spots.append(tuple(where))
    return array.at[spots[0]].set(low).at[spots[1]].set(top_value)


def levels(own_key, shape, cuts, low, largest):
    loudness = 1.0
    for dim, parts in cuts:
        heights = jax.random.uniform(jax.random.fold_in(jax.random.fold_in(own_key, 6), dim), (parts,), jnp.float32, low / len(cuts), largest / len(cuts))
        loudness = loudness * jnp.repeat(jnp.exp(heights), shape[dim] // parts).reshape((-1,) + (1,) * (len(shape) - 1 - dim))
    return loudness


def gaussian(own_key, dims, scale, limit, cuts=(), kind=jnp.bfloat16):
    values = jax.random.normal(own_key, dims, jnp.float32) * scale
    if len(cuts) > 0:
        values = levels(own_key, dims, cuts, -0.22, 0.18) * values
    return jnp.clip(values, min=-limit, max=limit).astype(kind)


def setup_inputs(seed: int = 0) -> dict:
    arg_keys = jax.random.split(jax.random.key(seed), 17)
    latents = gaussian(arg_keys[0], (NODES, D), 1.0, 6.0, ((0, 16), (1, 2)), jnp.float32)
    edge_latents = gaussian(arg_keys[1], (EDGES, D), 1.0, 6.0, ((0, 32),), jnp.float32)
    edge_sender = draw_edge_sender(jax.random.fold_in(arg_keys[16], 71), 0)
    edge_receiver = with_ends(jax.random.randint(arg_keys[3], (EDGES,), 0, NODE_DEV), jax.random.fold_in(arg_keys[3], 1), 0, NODE_DEV - 1).astype(jnp.int32)
    block_counts = draw_block_counts(jax.random.fold_in(arg_keys[16], 71), 0)
    send_rows = with_ends(jax.random.randint(arg_keys[5], (SHARDS, SHARDS, SLOT), 0, NODE_DEV), jax.random.fold_in(arg_keys[5], 1), 0, NODE_DEV - 1).astype(jnp.int32)
    edge_first_weight = gaussian(arg_keys[6], (LAYERS, 3 * D, HID), (3 * D) ** -0.5, 0.15625)
    edge_first_bias = gaussian(arg_keys[7], (LAYERS, HID), 0.5, 3.0, (), jnp.float32)
    edge_second_weight = draw_edge_second_weight(jax.random.fold_in(arg_keys[16], 71), 0)
    edge_gain = jnp.clip(1.0 + 0.18 * jax.random.normal(arg_keys[9], (LAYERS, D), jnp.float32), 0.1, 1.9)
    edge_offset = gaussian(arg_keys[10], (LAYERS, D), 0.5, 3.0, (), jnp.float32)
    node_first_weight = gaussian(arg_keys[11], (LAYERS, 2 * D, HID), (2 * D) ** -0.5, 0.1875)
    node_first_bias = gaussian(arg_keys[12], (LAYERS, HID), 0.5, 3.0, (), jnp.float32)
    node_second_weight = draw_node_second_weight(jax.random.fold_in(arg_keys[16], 71), 0)
    node_gain = jnp.clip(1.0 + 0.18 * jax.random.normal(arg_keys[14], (LAYERS, D), jnp.float32), 0.1, 1.9)
    node_offset = gaussian(arg_keys[15], (LAYERS, D), 0.5, 3.0, (), jnp.float32)
    return {"latents": latents, "edge_latents": edge_latents, "edge_sender": edge_sender, "edge_receiver": edge_receiver, "block_counts": block_counts, "send_rows": send_rows, "edge_first_weight": edge_first_weight, "edge_first_bias": edge_first_bias, "edge_second_weight": edge_second_weight, "edge_gain": edge_gain, "edge_offset": edge_offset, "node_first_weight": node_first_weight, "node_first_bias": node_first_bias, "node_second_weight": node_second_weight, "node_gain": node_gain, "node_offset": node_offset}


epsilon = 1e-05

def layer_norm(values, norm_gain, norm_offset):
    centre = values - lax.optimization_barrier(jnp.mean(values, axis=-1, keepdims=True))
    spread = lax.optimization_barrier(jnp.mean(centre * centre, axis=-1, keepdims=True))
    return centre * lax.rsqrt(spread + epsilon) * norm_gain + norm_offset

def perceptron(pieces, first_weight, first_bias, second_weight, norm_gain, norm_offset):
    columns = pieces[0].shape[1]
    running = first_bias
    for position in range(len(pieces)):
        running = running + jnp.dot(pieces[position], first_weight[position * columns:(position + 1) * columns], preferred_element_type=jnp.float32)
    active = (running * jax.nn.sigmoid(running)).astype(jnp.bfloat16)
    result = jnp.dot(active, second_weight, preferred_element_type=jnp.float32)
    return layer_norm(result, norm_gain, norm_offset)

def reference(latents, edge_latents, edge_sender, edge_receiver, block_counts, send_rows, edge_first_weight, edge_first_bias, edge_second_weight, edge_gain, edge_offset, node_first_weight, node_first_bias, node_second_weight, node_gain, node_offset):
    shards = NODES // NODE_DEV
    slot_index = jnp.arange(EDGES, dtype=jnp.int32)
    owning = slot_index // EDGE_DEV
    beyond = edge_sender - NODE_DEV
    source_shard = jnp.clip(beyond // SLOT, 0, shards - 1).astype(jnp.int32)
    slot_pos = jnp.clip(beyond % SLOT, 0, SLOT - 1).astype(jnp.int32)
    remote = source_shard * NODE_DEV + send_rows[source_shard, owning, slot_pos]
    senders = jnp.where(edge_sender < NODE_DEV, owning * NODE_DEV + edge_sender, remote).astype(jnp.int32)
    receivers = (owning * NODE_DEV + edge_receiver).astype(jnp.int32)
    usable = slot_index % BLOCK < block_counts[slot_index // BLOCK]
    node_state = latents
    edge_state = edge_latents
    for layer_index in range(LAYERS):
        node_low = node_state.astype(jnp.bfloat16)

        def portion(operands):
            edge_part, send_part, recv_part = operands
            return perceptron((edge_part.astype(jnp.bfloat16), node_low[send_part], node_low[recv_part]), edge_first_weight[layer_index], edge_first_bias[layer_index], edge_second_weight[layer_index], edge_gain[layer_index], edge_offset[layer_index])
        update = lax.map(portion, (edge_state.reshape(shards, EDGE_DEV, D), senders.reshape(shards, EDGE_DEV), receivers.reshape(shards, EDGE_DEV)))
        update = update.reshape(EDGES, D)
        edge_state = edge_state + jnp.where(usable[:, None], update, jnp.zeros_like(update))
        edge_out_low = lax.optimization_barrier(edge_state.astype(jnp.bfloat16)).astype(jnp.float32)
        summed = jax.ops.segment_sum(jnp.where(usable[:, None], edge_out_low, jnp.zeros_like(edge_out_low)), receivers, num_segments=NODES)
        summed_low = summed.astype(jnp.bfloat16)
        node_state = node_state + perceptron((node_low, summed_low), node_first_weight[layer_index], node_first_bias[layer_index], node_second_weight[layer_index], node_gain[layer_index], node_offset[layer_index])
    return (node_state, edge_state)
```

```python
import functools

import jax
import jax.numpy as jnp
from jax import lax
from jax.experimental import pallas as pl
from jax.experimental.pallas import tpu as pltpu
from jax.sharding import PartitionSpec as P

epsilon = 1e-05
MESH = pl.DeviceIdType.MESH
F32 = jnp.float32
BF16 = jnp.bfloat16


def dot(a, b):
    return jnp.dot(a, b, preferred_element_type=F32)


def layer_norm(values, gain, offset):
    centre = values - jnp.mean(values, axis=-1, keepdims=True)
    spread = jnp.mean(centre * centre, axis=-1, keepdims=True)
    return centre * lax.rsqrt(spread + epsilon) * gain + offset


def swish(v):
    return (v * jax.nn.sigmoid(v)).astype(BF16)


def one_hot(column, width):
    places = lax.broadcasted_iota(jnp.int32, (column.shape[0], width), 1)
    return jnp.where(places == column, 1.0, 0.0).astype(BF16)


def one_hot_rows(row, height):
    places = lax.broadcasted_iota(jnp.int32, (height, row.shape[1]), 0)
    return jnp.where(places == row, 1.0, 0.0).astype(BF16)


def local_hot(columns, nodes):
    sender, receiver = columns[:, 0:1], columns[:, 1:2]
    local = jnp.where(sender < nodes, sender, -1)
    places = lax.broadcasted_iota(jnp.int32, (columns.shape[0], 2 * nodes), 1)
    hit = (places == local) | (places == receiver + nodes)
    return jnp.where(hit, 1.0, 0.0).astype(BF16)


def finish_edges(pre, state, columns, row, halo_table, second, gain, offset, nodes):
    pre = pre + dot(one_hot(columns[:, 0:1] - nodes, halo_table.shape[0]), halo_table)
    update = layer_norm(dot(swish(pre), second), gain, offset)
    state = state + jnp.where(columns[:, 2:3] > 0, update, jnp.zeros_like(update))
    return state, dot(one_hot_rows(row, nodes), state.astype(BF16))


def node_update(node_low, summed, first, first_bias, second, gain, offset):
    width = node_low.shape[1]
    v = dot(node_low, first[0:width]) + dot(summed.astype(BF16), first[width:]) + first_bias
    return layer_norm(dot(swish(v), second), gain, offset)


def first_kernel(
    patches, bands, chunk,
    lat_ref, columns_ref, rows_ref, lists_ref, eb_ref, eg_ref, eo_ref, nb_ref, ng_ref, no_ref,
    edge_hbm, ew1_hbm, ew2_hbm, nw1_hbm, nw2_hbm,
    node_out, table_out, state_hbm, pre_hbm,
    state, pre, w1, w2, v1, v2, x1, low_out, low_in, wide_in, out_a, out_b, in_a, in_b, table, summed,
    load_sem, store_sem, low_send, low_recv, wide_send, wide_recv, send_a, recv_a, send_b, recv_b,
):
    shards = patches * bands
    patch, band = lax.axis_index("patch"), lax.axis_index("band")
    me = patch * bands + band
    nodes = node_out.shape[0]
    edges, width = state.shape
    chunks = edges // chunk
    slot = out_a.shape[1]

    loads = [
        pltpu.make_async_copy(src, dst, load_sem.at[i])
        for i, (src, dst) in enumerate((
            (edge_hbm, state), (ew1_hbm.at[0], w1), (ew2_hbm.at[0], w2),
            (nw1_hbm.at[0], v1), (nw2_hbm.at[0], v2), (ew1_hbm.at[1], x1),
        ))
    ]
    for load in (loads[1], loads[0], loads[2], loads[3], loads[4], loads[5]):
        load.start()

    def place(q):
        return (lax.div(q, bands), lax.rem(q, bands))

    barrier = pltpu.get_barrier_semaphore()

    def greet(i, c):
        pl.semaphore_signal(barrier, inc=1, device_id=place(lax.rem(me + i, shards)), device_id_type=MESH)
        return c

    lax.fori_loop(1, shards, greet, 0)
    low_out[...] = lat_ref[...].astype(BF16)
    mine = pl.ds(pl.multiple_of(band * nodes, nodes), nodes)
    low_in[band] = lat_ref[mine, :].astype(BF16)
    wide_in[band] = lat_ref[mine, :]
    pl.semaphore_wait(barrier, shards - 1)

    exchanges = []
    for src, dst, ss, rs in ((low_out, low_in, low_send, low_recv), (lat_ref, wide_in, wide_send, wide_recv)):
        group = []
        for i in range(1, bands):
            other = lax.rem(band + i, bands)
            copy = pltpu.make_async_remote_copy(
                src_ref=src.at[pl.ds(pl.multiple_of(other * nodes, nodes), nodes)],
                dst_ref=dst.at[band],
                send_sem=ss.at[i],
                recv_sem=rs.at[i],
                device_id=(patch, other),
                device_id_type=MESH,
            )
            copy.start()
            group.append(copy)
        exchanges.append(group)

    def part(c):
        return pl.ds(pl.multiple_of(c * chunk, chunk), chunk)

    loads[1].wait()
    loads[0].wait()

    def own_edges(c, carry):
        pre[part(c), :] = dot(state[part(c), :].astype(BF16), w1[0:width, :]) + eb_ref[0:1, :]
        return carry

    lax.fori_loop(0, chunks, own_edges, 0)

    for copy in exchanges[0]:
        copy.wait()
    node_low = jnp.concatenate([low_in[i] for i in range(bands)], axis=1)
    hot_lists = one_hot_rows(lists_ref[...], nodes)

    def transfer(i, out, inn, ss, rs):
        q = lax.rem(me + i, shards)
        return pltpu.make_async_remote_copy(
            src_ref=out.at[q],
            dst_ref=inn.at[me],
            send_sem=ss.at[i],
            recv_sem=rs.at[i],
            device_id=place(q),
            device_id_type=MESH,
        )

    def send_halo(node_low, out, inn, ss, rs):
        picked = lax.dot_general(hot_lists, node_low, (((0,), (0,)), ((), ())), preferred_element_type=F32)
        out[...] = picked.reshape(shards, slot, width).astype(BF16)
        inn[me] = out[me]

        def go(i, c):
            transfer(i, out, inn, ss, rs).start()
            return c

        lax.fori_loop(1, shards, go, 0)

    def await_halo(out, inn, ss, rs):
        def stop(i, c):
            transfer(i, out, inn, ss, rs).wait()
            return c

        lax.fori_loop(1, shards, stop, 0)
        return inn[...].astype(F32).reshape(shards * slot, width).astype(BF16)

    send_halo(node_low, out_a, in_a, send_a, recv_a)
    table[0:nodes, :] = dot(node_low, w1[width : 2 * width, :]).astype(BF16)
    table[nodes:, :] = dot(node_low, w1[2 * width :, :]).astype(BF16)

    def own_nodes(c, carry):
        pre[part(c), :] += dot(local_hot(columns_ref[part(c), :], nodes), table[...])
        return carry

    lax.fori_loop(0, chunks, own_nodes, 0)
    for load in loads[2:]:
        load.wait()
    halo = await_halo(out_a, in_a, send_a, recv_a)
    table_out[...] = dot(halo, w1[width : 2 * width, :]).astype(BF16)
    summed[...] = jnp.zeros_like(summed)

    def finish(c, carry):
        fresh, added = finish_edges(
            pre[part(c), :], state[part(c), :], columns_ref[part(c), :], rows_ref[c], table_out[...],
            w2[...], eg_ref[0:1, :], eo_ref[0:1, :], nodes,
        )
        state[part(c), :] = fresh
        summed[...] += added
        return carry

    lax.fori_loop(0, chunks, finish, 0)
    for copy in exchanges[1]:
        copy.wait()
    node_state = jnp.concatenate([wide_in[i] for i in range(bands)], axis=1) + node_update(
        node_low, summed[...], v1, nb_ref[0:1, :], v2[...], ng_ref[0:1, :], no_ref[0:1, :]
    )
    node_out[...] = node_state
    node_low = node_state.astype(BF16)
    send_halo(node_low, out_b, in_b, send_b, recv_b)
    save_state = pltpu.make_async_copy(state, state_hbm, store_sem.at[0])
    save_state.start()
    table[0:nodes, :] = dot(node_low, x1[width : 2 * width, :]).astype(BF16)
    table[nodes:, :] = dot(node_low, x1[2 * width :, :]).astype(BF16)

    def begin(c, carry):
        pre[part(c), :] = (
            dot(state[part(c), :].astype(BF16), x1[0:width, :])
            + eb_ref[1:2, :]
            + dot(local_hot(columns_ref[part(c), :], nodes), table[...])
        )
        return carry

    lax.fori_loop(0, chunks, begin, 0)
    save_pre = pltpu.make_async_copy(pre, pre_hbm, store_sem.at[1])
    save_pre.start()
    halo = await_halo(out_b, in_b, send_b, recv_b)
    table_out[...] = dot(halo, x1[width : 2 * width, :]).astype(BF16)
    save_state.wait()
    save_pre.wait()


def second_kernel(
    chunks,
    pre_ref, state_ref, columns_ref, rows_ref, table_ref, ew2_ref, eg_ref, eo_ref,
    node_ref, nw1_ref, nb_ref, nw2_ref, ng_ref, no_ref,
    nodes_out, edges_out,
    summed,
):
    step = pl.program_id(0)
    nodes = node_ref.shape[0]

    @pl.when(step == 0)
    def _():
        summed[...] = jnp.zeros_like(summed)

    fresh, added = finish_edges(
        pre_ref[...], state_ref[...], columns_ref[...], rows_ref[0], table_ref[...],
        ew2_ref[0], eg_ref[1:2, :], eo_ref[1:2, :], nodes,
    )
    edges_out[...] = fresh
    summed[...] += added

    @pl.when(step == chunks - 1)
    def _():
        old = node_ref[...]
        nodes_out[...] = old + node_update(
            old.astype(BF16), summed[...], nw1_ref.at[0], nb_ref[1:2, :], nw2_ref[0], ng_ref[1:2, :], no_ref[1:2, :]
        )


def shards_body(
    patches, bands,
    latents, edge_latents, edge_sender, edge_receiver, block_counts, send_rows,
    edge_first_weight, edge_first_bias, edge_second_weight, edge_gain, edge_offset,
    node_first_weight, node_first_bias, node_second_weight, node_gain, node_offset,
):
    shards = patches * bands
    edges, width = edge_latents.shape
    block = edges // block_counts.shape[0]
    nodes = latents.shape[0] // bands
    slot = send_rows.shape[2]
    chunk = next(c for c in (512, 256, 128, block) if edges % c == 0)
    chunks = edges // chunk
    usable = (jnp.arange(block, dtype=jnp.int32)[None, :] < block_counts[:, None]).reshape(-1)
    columns = jnp.stack([edge_sender, edge_receiver, usable.astype(jnp.int32)], axis=1)
    rows = jnp.where(usable, edge_receiver, -1).reshape(chunks, 1, chunk)
    lists = send_rows.reshape(1, shards * slot)
    vmem, anywhere = pl.BlockSpec(memory_space=pltpu.VMEM), pl.BlockSpec(memory_space=pl.ANY)
    dma = pltpu.SemaphoreType.DMA
    half = latents.shape[1]
    node_state, table, state, pre = pl.pallas_call(
        functools.partial(first_kernel, patches, bands, chunk),
        out_shape=(
            jax.ShapeDtypeStruct((nodes, width), F32),
            jax.ShapeDtypeStruct((shards * slot, width), BF16),
            jax.ShapeDtypeStruct((edges, width), F32),
            jax.ShapeDtypeStruct((edges, width), F32),
        ),
        in_specs=[vmem] * 10 + [anywhere] * 5,
        out_specs=(vmem, vmem, anywhere, anywhere),
        scratch_shapes=[
            pltpu.VMEM((edges, width), F32),
            pltpu.VMEM((edges, width), F32),
            pltpu.VMEM(edge_first_weight.shape[1:], BF16),
            pltpu.VMEM(edge_second_weight.shape[1:], BF16),
            pltpu.VMEM(node_first_weight.shape[1:], BF16),
            pltpu.VMEM(node_second_weight.shape[1:], BF16),
            pltpu.VMEM(edge_first_weight.shape[1:], BF16),
            pltpu.VMEM(latents.shape, BF16),
            pltpu.VMEM((bands, nodes, half), BF16),
            pltpu.VMEM((bands, nodes, half), F32),
            pltpu.VMEM((shards, slot, width), BF16),
            pltpu.VMEM((shards, slot, width), BF16),
            pltpu.VMEM((shards, slot, width), BF16),
            pltpu.VMEM((shards, slot, width), BF16),
            pltpu.VMEM((2 * nodes, width), BF16),
            pltpu.VMEM((nodes, width), F32),
            dma((6,)), dma((2,)),
            dma((bands,)), dma((bands,)), dma((bands,)), dma((bands,)),
            dma((shards,)), dma((shards,)), dma((shards,)), dma((shards,)),
        ],
        compiler_params=pltpu.CompilerParams(
            collective_id=0, has_side_effects=True, vmem_limit_bytes=48 * 2**20
        ),
        name="layer_one",
    )(
        latents, columns, rows, lists, edge_first_bias, edge_gain, edge_offset,
        node_first_bias, node_gain, node_offset,
        edge_latents, edge_first_weight, edge_second_weight, node_first_weight, node_second_weight,
    )

    def whole(array):
        return pl.BlockSpec(array.shape, lambda c: (0,) * array.ndim)

    def second(array):
        return pl.BlockSpec((1,) + array.shape[1:], lambda c: (1, 0, 0))

    def stream(columns):
        return pl.BlockSpec((chunk, columns), lambda c: (c, 0))

    return pl.pallas_call(
        functools.partial(second_kernel, chunks),
        grid=(chunks,),
        out_shape=(
            jax.ShapeDtypeStruct((nodes, width), F32),
            jax.ShapeDtypeStruct((edges, width), F32),
        ),
        in_specs=[
            stream(width), stream(width), stream(3), pl.BlockSpec((1, 1, chunk), lambda c: (c, 0, 0)),
            whole(table), second(edge_second_weight), whole(edge_gain), whole(edge_offset),
            whole(node_state), second(node_first_weight), whole(node_first_bias), second(node_second_weight),
            whole(node_gain), whole(node_offset),
        ],
        out_specs=(whole(node_state), stream(width)),
        scratch_shapes=[pltpu.VMEM((nodes, width), F32)],
        compiler_params=pltpu.CompilerParams(
            dimension_semantics=("arbitrary",), vmem_limit_bytes=48 * 2**20
        ),
        name="layer_two",
    )(
        pre, state, columns, rows, table, edge_second_weight, edge_gain, edge_offset,
        node_state, node_first_weight, node_first_bias, node_second_weight, node_gain, node_offset,
    )


def solution(mesh):
    owned = P(("patch", "band"))
    return jax.shard_map(
        functools.partial(shards_body, mesh.shape["patch"], mesh.shape["band"]),
        mesh=mesh,
        in_specs=(P("patch", "band"), owned, owned, owned, owned, owned) + (P(),) * 10,
        out_specs=(owned, owned),
        check_vma=False,
    )
```

```python
import functools

import jax
import jax.numpy as jnp
from jax import lax
from jax.experimental import pallas as pl
from jax.experimental.pallas import tpu as pltpu
from jax.sharding import PartitionSpec as P

epsilon = 1e-05
MESH = pl.DeviceIdType.MESH
F32 = jnp.float32
BF16 = jnp.bfloat16


def dot(a, b):
    return jnp.dot(a, b, preferred_element_type=F32)


def layer_norm(values, gain, offset):
    centre = values - jnp.mean(values, axis=-1, keepdims=True)
    spread = jnp.mean(centre * centre, axis=-1, keepdims=True)
    return centre * lax.rsqrt(spread + epsilon) * gain + offset


def swish(v):
    return (v * jax.nn.sigmoid(v)).astype(BF16)


LANES = 128


def hot_columns(conditions, width):
    places = lax.broadcasted_iota(jnp.int32, (conditions[0].shape[0], LANES), 1)
    pieces = []
    for first in range(0, width, LANES):
        hit = places == conditions[0] - first
        for other in conditions[1:]:
            hit = hit | (places == other - first)
        pieces.append(jnp.where(hit, 1.0, 0.0))
    return jnp.concatenate(pieces, axis=1).astype(BF16)


def one_hot_rows(row, height):
    places = lax.broadcasted_iota(jnp.int32, (height, row.shape[1]), 0)
    return jnp.where(places == row, 1.0, 0.0).astype(BF16)


def hot_columns_of(rows, width, step):
    row_place = lax.broadcasted_iota(jnp.int32, (rows, width), 0)
    column_place = lax.broadcasted_iota(jnp.int32, (rows, width), 1)
    return jnp.where(lax.div(row_place, step) == column_place, 1.0, 0.0).astype(BF16)


def to_columns(row):
    return jnp.broadcast_to(row, (row.shape[1], row.shape[1])).T


def used_row(row, count):
    places = lax.broadcasted_iota(jnp.int32, row.shape, 1)
    return jnp.where(places < count, row, -1)


def local_hot(sender, receiver, nodes):
    return hot_columns((jnp.where(sender < nodes, sender, -1), receiver + nodes), 2 * nodes)


def finish_edges(pre, state, sender, row, counts, halo_table, second, gain, offset, nodes):
    pre = pre + dot(hot_columns((sender - nodes,), halo_table.shape[0]), halo_table)
    update = layer_norm(dot(swish(pre), second), gain, offset)
    places = lax.broadcasted_iota(jnp.int32, (LANES, update.shape[1]), 0)
    kept = [
        jnp.where(places < count, update[i * LANES : (i + 1) * LANES], 0.0)
        for i, count in enumerate(counts)
    ]
    state = state + jnp.concatenate(kept, axis=0)
    return state, dot(one_hot_rows(row, nodes), state.astype(BF16))


def node_update(node_low, summed, first, first_bias, second, gain, offset):
    width = node_low.shape[1]
    v = dot(node_low, first[0:width]) + dot(summed.astype(BF16), first[width:]) + first_bias
    return layer_norm(dot(swish(v), second), gain, offset)


def first_kernel(
    patches, bands, chunk,
    counts_ref,
    lat_hbm, senders_hbm, receivers_hbm, lists_hbm, eb_hbm, eg_hbm, eo_hbm, nb_hbm, ng_hbm, no_hbm,
    edge_hbm, ew1_hbm, ew2_hbm, nw1_hbm, nw2_hbm,
    node_hbm, table_hbm, state_hbm, pre_hbm,
    lat_ref, senders_ref, receivers_ref, lists_ref, eb_ref, eg_ref, eo_ref, nb_ref, ng_ref, no_ref,
    node_out, table_out, sender_cols, receiver_cols, rows_ref,
    state, pre, w1, w2, v1, v2, x1, low_out, low_in, wide_in, out_a, out_b, in_a, in_b, table, summed,
    load_sem, store_sem, low_send, low_recv, wide_send, wide_recv, send_a, recv_a, send_b, recv_b,
):
    shards = patches * bands
    patch, band = lax.axis_index("patch"), lax.axis_index("band")
    me = patch * bands + band
    nodes = node_out.shape[0]
    edges, width = state.shape
    chunks = edges // chunk
    blocks = chunk // LANES
    slot = out_a.shape[1]

    loads = [
        pltpu.make_async_copy(src, dst, load_sem.at[i])
        for i, (src, dst) in enumerate((
            (edge_hbm, state), (ew1_hbm.at[0], w1), (ew2_hbm.at[0], w2),
            (nw1_hbm.at[0], v1), (nw2_hbm.at[0], v2), (ew1_hbm.at[1], x1),
            (lat_hbm, lat_ref), (senders_hbm, senders_ref), (receivers_hbm, receivers_ref),
            (lists_hbm.at[0], lists_ref), (eb_hbm, eb_ref), (eg_hbm, eg_ref), (eo_hbm, eo_ref),
            (nb_hbm, nb_ref), (ng_hbm, ng_ref), (no_hbm, no_ref),
        ))
    ]
    for load in [loads[i] for i in (6, 7, 8, 9, 10, 1, 0, 2, 3, 4, 5, 11, 12, 13, 14, 15)]:
        load.start()

    def place(q):
        return (lax.div(q, bands), lax.rem(q, bands))

    barrier = pltpu.get_barrier_semaphore()

    def greet(i, c):
        pl.semaphore_signal(barrier, inc=1, device_id=place(lax.rem(me + i, shards)), device_id_type=MESH)
        return c

    lax.fori_loop(1, shards, greet, 0)
    loads[6].wait()
    low_out[...] = lat_ref[...].astype(BF16)
    mine = pl.ds(pl.multiple_of(band * nodes, nodes), nodes)
    low_in[band] = lat_ref[mine, :].astype(BF16)
    wide_in[band] = lat_ref[mine, :]
    pl.semaphore_wait(barrier, shards - 1)

    exchanges = []
    for src, dst, ss, rs in ((low_out, low_in, low_send, low_recv), (lat_ref, wide_in, wide_send, wide_recv)):
        group = []
        for i in range(1, bands):
            other = lax.rem(band + i, bands)
            copy = pltpu.make_async_remote_copy(
                src_ref=src.at[pl.ds(pl.multiple_of(other * nodes, nodes), nodes)],
                dst_ref=dst.at[band],
                send_sem=ss.at[i],
                recv_sem=rs.at[i],
                device_id=(patch, other),
                device_id_type=MESH,
            )
            copy.start()
            group.append(copy)
        exchanges.append(group)

    def part(c):
        return pl.ds(pl.multiple_of(c * chunk, chunk), chunk)

    for load in loads[7:11]:
        load.wait()

    def turn(j, carry):
        here = pl.ds(pl.multiple_of(j * LANES, LANES), LANES)
        sender_cols[here, :] = to_columns(senders_ref[j])
        receiver_cols[here, :] = to_columns(receivers_ref[j])
        rows_ref[j] = used_row(receivers_ref[j], counts_ref[j])
        return carry

    lax.fori_loop(0, edges // LANES, turn, 0)
    lists = lists_ref[...]
    slots = lists.shape[1]
    spread = hot_columns_of(shards * slots, shards, slots)
    high = dot(spread, jnp.right_shift(lists, 4).astype(F32).astype(BF16))
    picked_all = high * 16.0 + dot(spread, jnp.bitwise_and(lists, 15).astype(F32).astype(BF16))
    row_place = lax.broadcasted_iota(jnp.int32, picked_all.shape, 0)
    slot_place = lax.broadcasted_iota(jnp.int32, picked_all.shape, 1)
    wanted = jnp.sum(
        jnp.where(lax.rem(row_place, slots) == slot_place, picked_all, 0.0), axis=1, keepdims=True
    )
    node_place = lax.broadcasted_iota(jnp.int32, (shards * slots, nodes), 1).astype(F32)
    hot_lists = jnp.where(node_place == wanted, 1.0, 0.0).astype(BF16)
    loads[1].wait()
    loads[0].wait()

    def own_edges(c, carry):
        pre[part(c), :] = dot(state[part(c), :].astype(BF16), w1[0:width, :]) + eb_ref[0:1, :]
        return carry

    lax.fori_loop(0, chunks, own_edges, 0)

    for copy in exchanges[0]:
        copy.wait()
    node_low = jnp.concatenate([low_in[i] for i in range(bands)], axis=1)

    def transfer(i, out, inn, ss, rs):
        q = lax.rem(me + i, shards)
        return pltpu.make_async_remote_copy(
            src_ref=out.at[q],
            dst_ref=inn.at[me],
            send_sem=ss.at[i],
            recv_sem=rs.at[i],
            device_id=place(q),
            device_id_type=MESH,
        )

    def send_halo(node_low, out, inn, ss, rs):
        picked = dot(hot_lists, node_low)
        out[...] = picked.reshape(shards, slot, width).astype(BF16)
        inn[me] = out[me]

        def go(i, c):
            transfer(i, out, inn, ss, rs).start()
            return c

        lax.fori_loop(1, shards, go, 0)

    def await_halo(out, inn, ss, rs):
        def stop(i, c):
            transfer(i, out, inn, ss, rs).wait()
            return c

        lax.fori_loop(1, shards, stop, 0)
        return inn[...].astype(F32).reshape(shards * slot, width).astype(BF16)

    send_halo(node_low, out_a, in_a, send_a, recv_a)
    table[0:nodes, :] = dot(node_low, w1[width : 2 * width, :]).astype(BF16)
    table[nodes:, :] = dot(node_low, w1[2 * width :, :]).astype(BF16)

    def own_nodes(c, carry):
        pre[part(c), :] += dot(local_hot(sender_cols[part(c), :], receiver_cols[part(c), :], nodes), table[...])
        return carry

    lax.fori_loop(0, chunks, own_nodes, 0)
    for load in loads[2:6] + loads[11:]:
        load.wait()
    halo = await_halo(out_a, in_a, send_a, recv_a)
    table_out[...] = dot(halo, w1[width : 2 * width, :]).astype(BF16)
    summed[...] = jnp.zeros_like(summed)

    def finish(c, carry):
        fresh, added = finish_edges(
            pre[part(c), :], state[part(c), :], sender_cols[part(c), :],
            jnp.concatenate([rows_ref[c * blocks + i] for i in range(blocks)], axis=1),
            [counts_ref[c * blocks + i] for i in range(blocks)], table_out[...],
            w2[...], eg_ref[0:1, :], eo_ref[0:1, :], nodes,
        )
        state[part(c), :] = fresh
        summed[...] += added
        return carry

    lax.fori_loop(0, chunks, finish, 0)
    for copy in exchanges[1]:
        copy.wait()
    node_state = jnp.concatenate([wide_in[i] for i in range(bands)], axis=1) + node_update(
        node_low, summed[...], v1, nb_ref[0:1, :], v2[...], ng_ref[0:1, :], no_ref[0:1, :]
    )
    node_out[...] = node_state
    save_nodes = pltpu.make_async_copy(node_out, node_hbm, store_sem.at[2])
    save_nodes.start()
    node_low = node_state.astype(BF16)
    send_halo(node_low, out_b, in_b, send_b, recv_b)
    save_state = pltpu.make_async_copy(state, state_hbm, store_sem.at[0])
    save_state.start()
    table[0:nodes, :] = dot(node_low, x1[width : 2 * width, :]).astype(BF16)
    table[nodes:, :] = dot(node_low, x1[2 * width :, :]).astype(BF16)

    def begin(c, carry):
        pre[part(c), :] = (
            dot(state[part(c), :].astype(BF16), x1[0:width, :])
            + eb_ref[1:2, :]
            + dot(local_hot(sender_cols[part(c), :], receiver_cols[part(c), :], nodes), table[...])
        )
        return carry

    lax.fori_loop(0, chunks, begin, 0)
    save_pre = pltpu.make_async_copy(pre, pre_hbm, store_sem.at[1])
    save_pre.start()
    halo = await_halo(out_b, in_b, send_b, recv_b)
    table_out[...] = dot(halo, x1[width : 2 * width, :]).astype(BF16)
    save_table = pltpu.make_async_copy(table_out, table_hbm, store_sem.at[3])
    save_table.start()
    for save in (save_nodes, save_state, save_pre, save_table):
        save.wait()


def second_kernel(
    chunks,
    counts_ref, pre_ref, state_ref, senders_ref, receivers_ref, table_ref, ew2_ref, eg_ref, eo_ref,
    node_ref, nw1_ref, nb_ref, nw2_ref, ng_ref, no_ref,
    nodes_out, edges_out,
    summed,
):
    step = pl.program_id(0)
    nodes = node_ref.shape[0]

    @pl.when(step == 0)
    def _():
        summed[...] = jnp.zeros_like(summed)

    blocks = senders_ref.shape[0]
    counts = [counts_ref[step * blocks + i] for i in range(blocks)]
    fresh, added = finish_edges(
        pre_ref[...], state_ref[...],
        jnp.concatenate([to_columns(senders_ref[i]) for i in range(blocks)], axis=0),
        jnp.concatenate([used_row(receivers_ref[i], counts[i]) for i in range(blocks)], axis=1),
        counts, table_ref[...],
        ew2_ref[0], eg_ref[1:2, :], eo_ref[1:2, :], nodes,
    )
    edges_out[...] = fresh
    summed[...] += added

    @pl.when(step == chunks - 1)
    def _():
        old = node_ref[...]
        nodes_out[...] = old + node_update(
            old.astype(BF16), summed[...], nw1_ref.at[0], nb_ref[1:2, :], nw2_ref[0], ng_ref[1:2, :], no_ref[1:2, :]
        )


def shards_body(
    patches, bands,
    latents, edge_latents, edge_sender, edge_receiver, block_counts, send_rows,
    edge_first_weight, edge_first_bias, edge_second_weight, edge_gain, edge_offset,
    node_first_weight, node_first_bias, node_second_weight, node_gain, node_offset,
):
    shards = patches * bands
    edges, width = edge_latents.shape
    block = edges // block_counts.shape[0]
    nodes = latents.shape[0] // bands
    slot = send_rows.shape[2]
    chunk = next(c for c in (512, 256, 128) if edges % c == 0 and block == LANES)
    chunks = edges // chunk
    senders = edge_sender.reshape(edges // LANES, 1, LANES)
    receivers = edge_receiver.reshape(edges // LANES, 1, LANES)
    scalars, anywhere = pl.BlockSpec(memory_space=pltpu.SMEM), pl.BlockSpec(memory_space=pl.ANY)
    dma = pltpu.SemaphoreType.DMA
    half = latents.shape[1]
    node_state, table, state, pre = pl.pallas_call(
        functools.partial(first_kernel, patches, bands, chunk),
        out_shape=(
            jax.ShapeDtypeStruct((nodes, width), F32),
            jax.ShapeDtypeStruct((shards * slot, width), BF16),
            jax.ShapeDtypeStruct((edges, width), F32),
            jax.ShapeDtypeStruct((edges, width), F32),
        ),
        in_specs=[scalars] + [anywhere] * 15,
        out_specs=(anywhere,) * 4,
        scratch_shapes=[
            pltpu.VMEM(latents.shape, F32),
            pltpu.VMEM(senders.shape, jnp.int32),
            pltpu.VMEM(senders.shape, jnp.int32),
            pltpu.VMEM(send_rows.shape[1:], jnp.int32),
        ] + [pltpu.VMEM(edge_gain.shape, F32)] * 6 + [
            pltpu.VMEM((nodes, width), F32),
            pltpu.VMEM((shards * slot, width), BF16),
            pltpu.VMEM((edges, LANES), jnp.int32),
            pltpu.VMEM((edges, LANES), jnp.int32),
            pltpu.VMEM(senders.shape, jnp.int32),
            pltpu.VMEM((edges, width), F32),
            pltpu.VMEM((edges, width), F32),
            pltpu.VMEM(edge_first_weight.shape[1:], BF16),
            pltpu.VMEM(edge_second_weight.shape[1:], BF16),
            pltpu.VMEM(node_first_weight.shape[1:], BF16),
            pltpu.VMEM(node_second_weight.shape[1:], BF16),
            pltpu.VMEM(edge_first_weight.shape[1:], BF16),
            pltpu.VMEM(latents.shape, BF16),
            pltpu.VMEM((bands, nodes, half), BF16),
            pltpu.VMEM((bands, nodes, half), F32),
            pltpu.VMEM((shards, slot, width), BF16),
            pltpu.VMEM((shards, slot, width), BF16),
            pltpu.VMEM((shards, slot, width), BF16),
            pltpu.VMEM((shards, slot, width), BF16),
            pltpu.VMEM((2 * nodes, width), BF16),
            pltpu.VMEM((nodes, width), F32),
            dma((16,)), dma((4,)),
            dma((bands,)), dma((bands,)), dma((bands,)), dma((bands,)),
            dma((shards,)), dma((shards,)), dma((shards,)), dma((shards,)),
        ],
        compiler_params=pltpu.CompilerParams(
            collective_id=0, has_side_effects=True, vmem_limit_bytes=67043328
        ),
        name="layer_one",
    )(
        block_counts, latents, senders, receivers, send_rows, edge_first_bias, edge_gain, edge_offset,
        node_first_bias, node_gain, node_offset,
        edge_latents, edge_first_weight, edge_second_weight, node_first_weight, node_second_weight,
    )

    def whole(array):
        return pl.BlockSpec(array.shape, lambda c: (0,) * array.ndim)

    def second(array):
        return pl.BlockSpec((1,) + array.shape[1:], lambda c: (1, 0, 0))

    def stream(columns):
        return pl.BlockSpec((chunk, columns), lambda c: (c, 0))

    indices = pl.BlockSpec((chunk // LANES, 1, LANES), lambda c: (c, 0, 0))
    return pl.pallas_call(
        functools.partial(second_kernel, chunks),
        grid=(chunks,),
        out_shape=(
            jax.ShapeDtypeStruct((nodes, width), F32),
            jax.ShapeDtypeStruct((edges, width), F32),
        ),
        in_specs=[
            scalars, stream(width), stream(width), indices, indices,
            whole(table), second(edge_second_weight), whole(edge_gain), whole(edge_offset),
            whole(node_state), second(node_first_weight), whole(node_first_bias), second(node_second_weight),
            whole(node_gain), whole(node_offset),
        ],
        out_specs=(whole(node_state), stream(width)),
        scratch_shapes=[pltpu.VMEM((nodes, width), F32)],
        compiler_params=pltpu.CompilerParams(
            dimension_semantics=("arbitrary",), vmem_limit_bytes=67043328
        ),
        name="layer_two",
    )(
        block_counts, pre, state, senders, receivers, table, edge_second_weight, edge_gain, edge_offset,
        node_state, node_first_weight, node_first_bias, node_second_weight, node_gain, node_offset,
    )


def solution(mesh):
    owned = P(("patch", "band"))
    return jax.shard_map(
        functools.partial(shards_body, mesh.shape["patch"], mesh.shape["band"]),
        mesh=mesh,
        in_specs=(P("patch", "band"), owned, owned, owned, owned, owned) + (P(),) * 10,
        out_specs=(owned, owned),
        check_vma=False,
    )
```
